32 devices in a mesh: pm: 2 (over x), ka: 8 (over z, core), isdf: 2 (over y).
Axes of the slice: x: 2, y: 2, z: 4, core: 2. Of those that a mesh axis runs over, the one named last changes fastest.
Arguments:
- amplitudes: bfloat16 [2, 2, 2, 16, 64, 256], P('pm', None, None, 'ka'), may hold values from -6 to 6
- conduction: bfloat16 [2, 16, 256, 512], P(None, 'ka', None, 'isdf'), may hold values from -0.375 to 0.375
- valence: bfloat16 [2, 16, 64, 512], P(None, 'ka'), may hold values from -0.75 to 0.75
- energy: float32 [16, 64, 256], P('ka', None, 'isdf'), may hold values from 0.5 to 2.5
- screened: bfloat16 [4, 2, 512, 512], P(None, None, 'isdf'), may hold values from -0.59765625 to 0.59765625
- coulomb: float32 [512, 512], P(None, 'isdf'), may hold values from -0.125 to 0.125
- mirror: int32 [16], P('ka'), may hold values from 0 to 15, as said below
- transfer_class: int32 [16, 16], P('ka'), may hold values from 0 to 3, as said below
Outputs:
- response: bfloat16 [2, 2, 2, 16, 64, 256], P('pm', None, None, 'ka', None, 'isdf')
The draws below stay inside these ranges and needn't reach their ends.
Inputs may be any that keep to these rules, and one draw needn't show every extreme that they name: mirror[mirror[k]] = k; a k-point of block j (the aligned block of 2 k-points that holds it) has its mirror in block 7 - j. transfer_class[k, k2] depends only on (k - k2) mod 16.
All inputs are finite; a program needn't handle non-finite values.
Results may differ from the reference program's by a relative error of at most 0.015.
Values may be sent and summed in bfloat16 or wider, within the bound.
No kernel may reach another device: no remote copies, remote signals or barrier semaphores. Data moves between devices by JAX's collectives and lax.ppermute only.
A program may use at most 128 MiB of HBM per device.

```python
import jax
import jax.numpy as jnp
from jax import lax

NV = 64
NC = 256
NISDF = 512
VECS = 2
KDEV = 2
WBLOCKS = 4
REACH = 2
NBLK = 8
NK = 16


def draw_mirror(key, part):
    block_count = NK // KDEV
    block_keys = jax.random.split(jax.random.fold_in(key, 5), block_count)
    orderings = jax.vmap(lambda subkey: jax.random.permutation(subkey, KDEV))(block_keys).astype(jnp.int32)
    inverses = jnp.argsort(orderings, axis=1, stable=True).astype(jnp.int32)
    blocks = jnp.arange(block_count, dtype=jnp.int32)
    opposite = (block_count - 1 - blocks).astype(jnp.int32)
    nearer = jnp.minimum(blocks, opposite).astype(jnp.int32)
    forward = jnp.take(orderings, nearer, axis=0)
    backward = jnp.take(inverses, nearer, axis=0)
    within = jnp.where((blocks < opposite)[:, None], forward, backward)
    return (opposite[:, None] * KDEV + within).reshape(NK).astype(jnp.int32)


def draw_transfer_class(key, part):
    class_key, order_key = jax.random.split(jax.random.fold_in(key, 17))
    classes = jax.random.randint(class_key, (NK,), 0, WBLOCKS, dtype=jnp.int32)
    classes = classes.at[:WBLOCKS].set(jax.random.permutation(order_key, WBLOCKS).astype(jnp.int32))
    points = jnp.arange(NK, dtype=jnp.int32)
    differ = jnp.mod(points[:, None] - points[None, :], NK)
    return jnp.take(classes, differ, axis=0).astype(jnp.int32)


def level_of(stream_key, dims, pieces, low, high):
    factor_of, own = 1.0, jax.random.fold_in(stream_key, 6)
    for dim, shards_of in pieces:
        heights = jnp.exp(jax.random.uniform(jax.random.fold_in(own, dim), (shards_of,), jnp.float32, low / len(pieces), high / len(pieces)))
        factor_of = factor_of * jnp.repeat(heights, dims[dim] // shards_of).reshape([-1 if axis == dim else 1 for axis in range(len(dims))])
    return factor_of


def centred(key, extent, deviation, bound, shards=(), kind=jnp.bfloat16):
    gain = level_of(key, extent, shards, -0.22, 0.18) if shards else 1.0
    values = jax.random.normal(key, extent, jnp.float32) * deviation * gain
    return jnp.minimum(jnp.maximum(values, -bound), bound).astype(kind)


def setup_inputs(seed: int = 0) -> dict:
    streams_of = jax.random.split(jax.random.key(seed), 9)
    return {
        "amplitudes": centred(streams_of[0], (2, VECS, 2, NK, NV, NC), 1.0, 6.0, ((0, 2), (3, 8))),
        "conduction": centred(streams_of[1], (2, NK, NC, NISDF), NC ** -0.5, 0.375, ((1, 8), (3, 2))),
        "valence": centred(streams_of[2], (2, NK, NV, NISDF), NV ** -0.5, 0.75, ((1, 8),)),
        "energy": jnp.clip(0.5 + 2.0 * jax.random.uniform(streams_of[3], (NK, NV, NC), jnp.float32) ** level_of(streams_of[3], (NK, NV, NC), ((0, 8), (2, 2)), -0.2, 0.2), 0.5, 2.5),
        "screened": centred(streams_of[4], (WBLOCKS, 2, NISDF, NISDF), 0.1, 0.59765625, ((2, 2),)),
        "coulomb": centred(streams_of[5], (NISDF, NISDF), (NISDF * NK // 4) ** -0.5, 0.125, ((1, 2),), jnp.float32),
        "mirror": draw_mirror(jax.random.fold_in(streams_of[8], 71), 0),
        "transfer_class": draw_transfer_class(jax.random.fold_in(streams_of[8], 71), 0),
    }


HIGHEST = lax.Precision.HIGHEST


def pair_einsum(pattern, left, right, conjugate):
    def single(first, second):
        return jnp.einsum(pattern, first.astype(jnp.float32), second.astype(jnp.float32), precision=HIGHEST)

    if conjugate:
        real_part = single(left[0], right[0]) + single(left[1], right[1])
        imag_part = single(left[1], right[0]) - single(left[0], right[1])
    else:
        real_part = single(left[0], right[0]) - single(left[1], right[1])
        imag_part = single(left[0], right[1]) + single(left[1], right[0])
    return real_part, imag_part


def conjugated(field):
    return jnp.stack([field[:, 0], -field[:, 1]], axis=1)


def channel(vector, conduction, valence, energy, screened, coulomb, transfer_class, weight):
    coef_real, coef_imag = pair_einsum("bkvc,kcm->bkvm", (vector[:, 0], vector[:, 1]), (conduction[0], conduction[1]), False)
    coef_real = coef_real.astype(jnp.bfloat16)
    coef_imag = coef_imag.astype(jnp.bfloat16)
    valence_real = valence[0].astype(jnp.float32)[None]
    valence_imag = valence[1].astype(jnp.float32)[None]
    coef_real_wide = coef_real.astype(jnp.float32)
    coef_imag_wide = coef_imag.astype(jnp.float32)
    rho_real = jnp.sum(valence_real * coef_real_wide + valence_imag * coef_imag_wide, axis=(1, 2))
    rho_imag = jnp.sum(valence_real * coef_imag_wide - valence_imag * coef_real_wide, axis=(1, 2))
    density = jnp.stack([rho_real, rho_imag], axis=1)
    potential = jnp.einsum("mn,brn->brm", coulomb, density, precision=HIGHEST)

    coef_by_point = jnp.moveaxis(jnp.stack([coef_real, coef_imag], axis=2), 1, 0)
    valence_by_point = jnp.moveaxis(valence, 1, 0)

    def pair_matrix(operands):
        coef_one, valence_one = operands
        real_part, imag_part = pair_einsum("bvm,vn->bmn", (coef_one[:, 0], coef_one[:, 1]), (valence_one[0], valence_one[1]), True)
        return jnp.stack([real_part, imag_part], axis=1).astype(jnp.bfloat16)

    matrices = lax.map(pair_matrix, (coef_by_point, valence_by_point))

    def block_product(block_id):
        first_point = (block_id * KDEV).astype(jnp.int32)
        total_real = jnp.zeros((VECS, KDEV, NISDF, NISDF), jnp.float32)
        total_imag = jnp.zeros((VECS, KDEV, NISDF, NISDF), jnp.float32)
        for offset in range(-REACH, REACH + 1):
            source = ((block_id + offset) % NBLK).astype(jnp.int32)
            source_point = (source * KDEV).astype(jnp.int32)
            visiting = lax.dynamic_slice_in_dim(matrices, source_point, KDEV, 0).astype(jnp.float32)
            classes = lax.dynamic_slice(transfer_class, (first_point, source_point), (KDEV, KDEV))
            chosen = jnp.take(screened, classes, axis=0).astype(jnp.float32)
            screen_real = chosen[:, :, 0][None]
            screen_imag = chosen[:, :, 1][None]
            pair_real = jnp.moveaxis(visiting[:, :, 0], 0, 1)[:, None]
            pair_imag = jnp.moveaxis(visiting[:, :, 1], 0, 1)[:, None]
            total_real = total_real + jnp.sum(screen_real * pair_real - screen_imag * pair_imag, axis=2)
            total_imag = total_imag + jnp.sum(screen_real * pair_imag + screen_imag * pair_real, axis=2)
        sum_real = total_real.astype(jnp.bfloat16)
        sum_imag = total_imag.astype(jnp.bfloat16)
        valence_block = lax.dynamic_slice_in_dim(valence, first_point, KDEV, 1)
        back_real, back_imag = pair_einsum("bkmn,kvn->bkvm", (sum_real, sum_imag), (valence_block[0], valence_block[1]), False)
        potential_real = potential[:, 0][:, None, None, :]
        potential_imag = potential[:, 1][:, None, None, :]
        block_real = valence_block[0].astype(jnp.float32)[None]
        block_imag = valence_block[1].astype(jnp.float32)[None]
        exchange_real = potential_real * block_real - potential_imag * block_imag
        exchange_imag = potential_real * block_imag + potential_imag * block_real
        field_real = (weight * exchange_real - back_real).astype(jnp.bfloat16)
        field_imag = (weight * exchange_imag - back_imag).astype(jnp.bfloat16)
        conduction_block = lax.dynamic_slice_in_dim(conduction, first_point, KDEV, 1)
        out_real, out_imag = pair_einsum("bkvm,kcm->bkvc", (field_real, field_imag), (conduction_block[0], conduction_block[1]), True)
        vector_block = lax.dynamic_slice_in_dim(vector, first_point, KDEV, 2).astype(jnp.float32)
        energy_block = lax.dynamic_slice_in_dim(energy, first_point, KDEV, 0)
        result = energy_block[None, None] * vector_block + jnp.stack([out_real, out_imag], axis=1)
        return result.astype(jnp.bfloat16)

    blocks = lax.map(block_product, jnp.arange(NBLK, dtype=jnp.int32))
    return jnp.moveaxis(blocks, 0, 2).reshape(VECS, 2, NK, NV, NC)


def reference(amplitudes, conduction, valence, energy, screened, coulomb, mirror, transfer_class):
    direct = amplitudes[0].astype(jnp.float32)
    flipped = conjugated(jnp.take(amplitudes[1], mirror, axis=2).astype(jnp.float32))
    plus_vector = (direct + flipped).astype(jnp.bfloat16)
    minus_vector = (direct - flipped).astype(jnp.bfloat16)
    plus_out = channel(plus_vector, conduction, valence, energy, screened, coulomb, transfer_class, 4.0).astype(jnp.float32)
    minus_out = channel(minus_vector, conduction, valence, energy, screened, coulomb, transfer_class, 0.0).astype(jnp.float32)
    first_half = (0.5 * (plus_out + minus_out)).astype(jnp.bfloat16)
    second_half = conjugated(jnp.take(0.5 * (plus_out - minus_out), mirror, axis=2)).astype(jnp.bfloat16)
    return jnp.stack([first_half, second_half], axis=0)
```

```python
import functools

import jax
import jax.numpy as jnp
from jax import lax
from jax.experimental import pallas as pl
from jax.experimental.pallas import tpu as pltpu
from jax.sharding import PartitionSpec as P

REACH = 2
F32 = jnp.float32
BF16 = jnp.bfloat16
HIGHEST = lax.Precision.HIGHEST
EXCHANGE = 2.0

SMEM = pl.BlockSpec(memory_space=pltpu.SMEM)
VMEM = pl.BlockSpec(memory_space=pltpu.VMEM)


def route(axis, target):
    return [(i, target(i)) for i in range(lax.axis_size(axis))]


def exchanged(value, axis, bit):
    return lax.ppermute(value, axis, route(axis, lambda i: i ^ bit))


def group_shift(value, by):
    count = lax.axis_size("ka")
    return lax.ppermute(value, "ka", route("ka", lambda i: (i + by * REACH) % count))


def reflected_block(value):
    count = lax.axis_size("ka")
    return lax.ppermute(value, ("pm", "ka"), [(count + i, 2 * count - 1 - i) for i in range(count)])


def nt_dot(left, right):
    return lax.dot_general(left, right, (((1,), (1,)), ((), ())), preferred_element_type=F32)


def coef_kernel(scal, amps, far, cond, val, keep, send, rho, whole):
    vectors, _, kpts, nv, nc = amps.shape
    mu = cond.shape[3]
    half = mu // REACH
    second = scal[0] == 1
    sign = jnp.where(second, -1.0, 1.0).astype(F32)
    first = pl.multiple_of(scal[1] * half, half)
    other = pl.multiple_of((1 - scal[1]) * half, half)
    for b in range(vectors):
        rho_r = jnp.zeros((1, mu), F32)
        rho_i = jnp.zeros((1, mu), F32)
        for k in range(kpts):
            near = amps[b, :, k].reshape(2 * nv, nc)
            away = far[b, :, scal[3 + k]].reshape(2 * nv, nc)
            z = jnp.where(second, away, near)
            by_r = jnp.dot(z, cond[0, k], preferred_element_type=F32)
            by_i = jnp.dot(z, cond[1, k], preferred_element_type=F32)
            g_r = by_r[:nv] - sign * by_i[nv:]
            g_i = by_i[:nv] + sign * by_r[nv:]
            v_r = val[0, k].astype(F32)
            v_i = val[1, k].astype(F32)
            rho_r = rho_r + jnp.sum(v_r * g_r + v_i * g_i, axis=0, keepdims=True)
            rho_i = rho_i + jnp.sum(v_r * g_i - v_i * g_r, axis=0, keepdims=True)
            whole[...] = jnp.concatenate([g_r, g_i], axis=0).T
            keep[b, k] = whole[pl.ds(first, half), :].astype(BF16)
            send[b, k] = whole[pl.ds(other, half), :].astype(BF16)
        rho[2 * b : 2 * b + 1, :] = rho_r
        rho[2 * b + 1 : 2 * b + 2, :] = rho_i


def screened_kernel(scal, classes, *refs, kpts, reach, rows):
    count = 3 * reach
    coefs = refs[:count]
    vals = refs[count : 2 * count]
    screen = refs[2 * count]
    outs = refs[2 * count + 1 : 2 * count + 1 + reach]
    pairs, sums, backs = refs[2 * count + 1 + reach :]
    vectors = coefs[0].shape[0]
    half, width = coefs[0].shape[2:]
    tile = screen.shape[3]
    total = classes.shape[1]
    step = pl.program_id(0)
    base = scal[0] * kpts

    def orbitals(block, k):
        v_r = vals[block][0, k]
        v_i = vals[block][1, k]
        return jnp.concatenate(
            [jnp.concatenate([v_r, -v_i], axis=1), jnp.concatenate([v_i, v_r], axis=1)], axis=0
        )

    @pl.when(step == 0)
    def _():
        backs[...] = jnp.zeros_like(backs)

    for block in range(count):
        for k in range(kpts):
            coef = coefs[block][:, k].reshape(vectors * half, width)
            made = jnp.dot(coef, orbitals(block, k), preferred_element_type=F32)
            pairs[block * kpts + k] = made.astype(BF16)

    widest = (reach + 1) * kpts - 1
    class_of = {d: classes[0, lax.rem(base - d + total, total)] for d in range(-widest, widest + 1)}

    def chunk(index, carry):
        row = pl.multiple_of(index * rows, rows)
        w_r = {d: screen[class_of[d], 0, pl.ds(row, rows), :] for d in class_of}
        w_i = {d: screen[class_of[d], 1, pl.ds(row, rows), :] for d in class_of}
        for b in range(vectors):
            place = pl.ds(pl.multiple_of(b * half + row, rows), rows)
            m_r = [pairs[p, place, :tile] for p in range(count * kpts)]
            m_i = [pairs[p, place, tile:] for p in range(count * kpts)]
            for point in range(reach * kpts):
                here = reach * kpts + point
                block = here // kpts
                real = imag = None
                for part in (0, 1):
                    part_r = part_i = None
                    for p in range((block - reach) * kpts, (block + reach + 1) * kpts):
                        if p % 2 != part:
                            continue
                        d = here - p
                        t_r = w_r[d] * m_r[p] - w_i[d] * m_i[p]
                        t_i = w_r[d] * m_i[p] + w_i[d] * m_r[p]
                        part_r = t_r if part_r is None else part_r + t_r
                        part_i = t_i if part_i is None else part_i + t_i
                    part_r = part_r.astype(F32)
                    part_i = part_i.astype(F32)
                    real = part_r if real is None else real + part_r
                    imag = part_i if imag is None else imag + part_i
                sums[point, place, :tile] = real.astype(BF16)
                sums[point, place, tile:] = imag.astype(BF16)
        return carry

    lax.fori_loop(0, half // rows, chunk, 0)

    for point in range(reach * kpts):
        block, k = divmod(point, kpts)
        backs[point] += nt_dot(sums[point], orbitals(reach + block, k))

    @pl.when(step == pl.num_programs(0) - 1)
    def _():
        mine = scal[1]
        for k in range(kpts):
            for choice in range(reach):
                picked = jnp.where(mine == 0, backs[choice * kpts + k], backs[(reach - 1 - choice) * kpts + k])
                outs[choice][:, k] = picked.reshape(vectors, half, width).astype(BF16)


def output_kernel(scal, own, got, cond, val, part, far_part, keep, send):
    vectors, kpts, half, width = own.shape
    nv = width // 2
    share = keep.shape[4]
    nc = cond.shape[2]
    low = scal[1] == 0
    side = scal[2] == 0
    spread = EXCHANGE * (part[...] + far_part[...])
    for k in range(kpts):
        fields = []
        for b in range(vectors):
            mine = own[b, k].astype(F32).T
            theirs = got[b, k].astype(F32).T
            back = jnp.concatenate([jnp.where(low, mine, theirs), jnp.where(low, theirs, mine)], axis=1)
            v_r = val[0, k].astype(F32)
            v_i = val[1, k].astype(F32)
            u_r = spread[2 * b : 2 * b + 1]
            u_i = spread[2 * b + 1 : 2 * b + 2]
            fields += [u_r * v_r - u_i * v_i - back[:nv], u_r * v_i + u_i * v_r - back[nv:]]
        field = jnp.concatenate(fields, axis=0).astype(BF16)
        by_r = nt_dot(field, cond[0, k])
        by_i = nt_dot(field, cond[1, k])
        for b in range(vectors):
            at = 2 * b * nv
            out_r = by_r[at : at + nv] + by_i[at + nv : at + 2 * nv]
            out_i = by_r[at + nv : at + 2 * nv] - by_i[at : at + nv]
            for ri, out in ((0, out_r), (1, out_i)):
                left, right = out[:, :share], out[:, share:]
                keep[b, ri, k] = jnp.where(side, left, right)
                send[b, ri, k] = jnp.where(side, right, left).astype(BF16)


def finish_kernel(scal, amps, far, energy, keep, got, out):
    vectors, _, kpts = amps.shape[:3]
    second = scal[0] == 1
    sign = jnp.where(second, -1.0, 1.0).astype(F32)
    for k in range(kpts):
        weight = energy[k]
        for b in range(vectors):
            for ri in range(2):
                near = amps[b, ri, k].astype(F32)
                away = far[b, ri, scal[3 + k]].astype(F32)
                z = jnp.where(second, away, near)
                if ri == 1:
                    z = sign * z
                out[b, ri, k] = (weight * z + keep[b, ri, k] + got[b, ri, k].astype(F32)).astype(BF16)


def place_kernel(scal, own, far, out):
    vectors, _, kpts = own.shape[:3]
    second = scal[0] == 1
    for k in range(kpts):
        for b in range(vectors):
            for ri in range(2):
                away = far[b, ri, scal[3 + k]]
                away = away if ri == 0 else -away
                out[b, ri, k] = jnp.where(second, away, own[b, ri, k])


def per_device(amplitudes, conduction, valence, energy, screened, coulomb, mirror, transfer_class):
    pm_index = lax.axis_index("pm")
    ka_index = lax.axis_index("ka")
    isdf_index = lax.axis_index("isdf")
    ka_count = lax.axis_size("ka")
    kpts = conduction.shape[1]
    nc = conduction.shape[2]
    mu = conduction.shape[3]
    points = valence.shape[3]
    nv = valence.shape[2]
    share = energy.shape[2]
    vectors = amplitudes.shape[1]
    half = mu // REACH
    width = 2 * nv
    local_mirror = jnp.clip(mirror - (ka_count - 1 - ka_index) * kpts, 0, kpts - 1)
    scal = jnp.concatenate(
        [jnp.stack([pm_index, ka_index % REACH, isdf_index]).astype(jnp.int32), local_mirror.astype(jnp.int32)]
    )
    near = amplitudes[0]
    far = reflected_block(near)

    val_pair = exchanged(valence, "ka", 1)
    val_above = group_shift(valence, -1)
    val_below = group_shift(valence, 1)
    val_above_pair = exchanged(val_above, "ka", 1)
    val_below_pair = exchanged(val_below, "ka", 1)

    coef_shape = (vectors, kpts, half, width)
    my_val = pl.BlockSpec((2, kpts, nv, mu), lambda i, s: (0, 0, 0, s[2]))

    def full(shape):
        return pl.BlockSpec(shape, lambda i, s: (0,) * len(shape))

    keep, send, rho = pl.pallas_call(
        coef_kernel,
        grid_spec=pltpu.PrefetchScalarGridSpec(
            num_scalar_prefetch=1,
            grid=(1,),
            in_specs=[full(near.shape), full(near.shape), full(conduction.shape), my_val],
            out_specs=[full(coef_shape), full(coef_shape), full((2 * vectors, mu))],
            scratch_shapes=[pltpu.VMEM((mu, width), F32)],
        ),
        out_shape=[
            jax.ShapeDtypeStruct(coef_shape, BF16),
            jax.ShapeDtypeStruct(coef_shape, BF16),
            jax.ShapeDtypeStruct((2 * vectors, mu), F32),
        ],
        name="coef",
    )(scal, near, far, conduction, valence)

    send_pair = exchanged(send, "ka", 1)
    above_send = group_shift(send, -1)
    below_send = group_shift(send, 1)
    above_keep = group_shift(keep, -1)
    below_keep = group_shift(keep, 1)
    above_pair = exchanged(above_send, "ka", 1)
    below_pair = exchanged(below_send, "ka", 1)

    total = rho
    bit = 1
    while bit < ka_count:
        total = total + exchanged(total, "ka", bit)
        bit *= 2
    total = total + exchanged(total, "pm", 1)
    part = jnp.einsum("nm,rm->rn", coulomb, total, precision=HIGHEST)
    far_part = exchanged(part, "isdf", 1)

    low = ka_index % REACH == 0

    def ordered(mine, theirs):
        return (jnp.where(low, mine, theirs), jnp.where(low, theirs, mine))

    coefs = (
        *ordered(below_keep, below_pair),
        *ordered(keep, send_pair),
        *ordered(above_keep, above_pair),
    )
    vals = (
        *ordered(val_below, val_below_pair),
        *ordered(valence, val_pair),
        *ordered(val_above, val_above_pair),
    )
    tile = 128
    grid = points // tile
    classes = screened.shape[0]
    body = functools.partial(screened_kernel, kpts=kpts, reach=REACH, rows=16)
    scal2 = jnp.stack([ka_index, ka_index % REACH]).astype(jnp.int32)
    mine, theirs = pl.pallas_call(
        body,
        grid_spec=pltpu.PrefetchScalarGridSpec(
            num_scalar_prefetch=2,
            grid=(grid,),
            in_specs=[pl.BlockSpec(coef_shape, lambda i, s, t: (0, 0, 0, 0))] * 6
            + [pl.BlockSpec((2, kpts, nv, tile), lambda i, s, t: (0, 0, 0, i))] * 6
            + [pl.BlockSpec((classes, 2, half, tile), lambda i, s, t: (0, 0, s[1], i))],
            out_specs=[pl.BlockSpec(coef_shape, lambda i, s, t: (0, 0, 0, 0))] * 2,
            scratch_shapes=[
                pltpu.VMEM((6 * kpts, vectors * half, 2 * tile), BF16),
                pltpu.VMEM((2 * kpts, vectors * half, 2 * tile), BF16),
                pltpu.VMEM((2 * kpts, vectors * half, width), F32),
            ],
        ),
        out_shape=[jax.ShapeDtypeStruct(coef_shape, BF16)] * 2,
        name="screen",
    )(scal2, transfer_class, *coefs, *vals, screened)
    got = exchanged(theirs, "ka", 1)

    out_shape = (vectors, 2, kpts, nv, share)
    my_part = pl.BlockSpec((2 * vectors, mu), lambda i, s: (0, s[2]))
    out_keep, out_send = pl.pallas_call(
        output_kernel,
        grid_spec=pltpu.PrefetchScalarGridSpec(
            num_scalar_prefetch=1,
            grid=(1,),
            in_specs=[
                full(coef_shape),
                full(coef_shape),
                full(conduction.shape),
                my_val,
                my_part,
                my_part,
            ],
            out_specs=[full(out_shape), full(out_shape)],
        ),
        out_shape=[jax.ShapeDtypeStruct(out_shape, F32), jax.ShapeDtypeStruct(out_shape, BF16)],
        name="output",
    )(scal, mine, got, conduction, valence, part, far_part)
    out_got = exchanged(out_send, "isdf", 1)
    amp_share = pl.BlockSpec(out_shape, lambda i, s: (0, 0, 0, 0, s[2]))
    channel = pl.pallas_call(
        finish_kernel,
        grid_spec=pltpu.PrefetchScalarGridSpec(
            num_scalar_prefetch=1,
            grid=(1,),
            in_specs=[amp_share, amp_share, full(energy.shape), full(out_shape), full(out_shape)],
            out_specs=full(out_shape),
        ),
        out_shape=jax.ShapeDtypeStruct(out_shape, BF16),
        name="finish",
    )(scal, near, far, energy, out_keep, out_got)
    distant = reflected_block(channel)
    result = pl.pallas_call(
        place_kernel,
        grid_spec=pltpu.PrefetchScalarGridSpec(
            num_scalar_prefetch=1,
            grid=(1,),
            in_specs=[full(out_shape), full(out_shape)],
            out_specs=full(out_shape),
        ),
        out_shape=jax.ShapeDtypeStruct(out_shape, BF16),
        name="place",
    )(scal, channel, distant)
    return result[None]


def solution(mesh):
    return jax.shard_map(
        per_device,
        mesh=mesh,
        in_specs=(
            P("pm", None, None, "ka", None, None),
            P(None, "ka", None, "isdf"),
            P(None, "ka", None, None),
            P("ka", None, "isdf"),
            P(None, None, "isdf", None),
            P(None, "isdf"),
            P("ka"),
            P("ka", None),
        ),
        out_specs=P("pm", None, None, "ka", None, "isdf"),
        check_vma=False,
    )
```

```python
import functools

import jax
import jax.numpy as jnp
from jax import lax
from jax.experimental import pallas as pl
from jax.experimental.pallas import tpu as pltpu
from jax.sharding import PartitionSpec as P


REACH = 2
F32 = jnp.float32
BF16 = jnp.bfloat16
HIGHEST = lax.Precision.HIGHEST
EXCHANGE = 2.0

SECOND, BASE, HALF, SIDE, MIRROR = range(5)

SMEM = pl.BlockSpec(memory_space=pltpu.SMEM)
VMEM = pl.BlockSpec(memory_space=pltpu.VMEM)


def route(axis, target):
    return [(i, target(i)) for i in range(lax.axis_size(axis))]


def exchanged(value, axis, bit):
    return lax.ppermute(value, axis, route(axis, lambda i: i ^ bit))


def group_shift(value, by):
    count = lax.axis_size("ka")
    return lax.ppermute(value, "ka", route("ka", lambda i: (i + by * REACH) % count))


def mirrored(value):
    count = lax.axis_size("ka")
    pairs = [(i, i) for i in range(count)] + [(count + i, 2 * count - 1 - i) for i in range(count)]
    return lax.ppermute(value, ("pm", "ka"), pairs)


def nt_dot(left, right, precision=None):
    return lax.dot_general(
        left, right, (((1,), (1,)), ((), ())), precision=precision, preferred_element_type=F32
    )


def copied(copies):
    for copy in copies:
        copy.start()
    for copy in copies:
        copy.wait()


def share_kernel(cond, val, cond_out, val_out, piece, sems):
    copied(
        [
            pltpu.make_async_copy(val.at[:, lax.axis_index("isdf")], piece, sems.at[0]),
            pltpu.make_async_copy(cond, cond_out, sems.at[1]),
            pltpu.make_async_copy(val, val_out, sems.at[2]),
        ]
    )


def stack_kernel(*refs):
    *values, out = refs
    for n, value in enumerate(values):
        out[n] = value[...]


def coef_kernel(scal, amps, cond, val, coefs, rho):
    vectors, _, kpts, nv, nc = amps.shape
    mu = cond.shape[3]
    half = mu // REACH
    sign = jnp.where(scal[SECOND] == 1, -1.0, 1.0).astype(F32)
    columns = pl.ds(pl.multiple_of(scal[SIDE] * mu, mu), mu)
    sums = [jnp.zeros((1, mu), F32) for _ in range(2 * vectors)]
    for k in range(kpts):
        z = amps[:, :, scal[MIRROR + k]].reshape(vectors * 2 * nv, nc)
        by_r = jnp.dot(z, cond[0, k], preferred_element_type=F32)
        by_i = jnp.dot(z, cond[1, k], preferred_element_type=F32)
        v_r = val[0, k, :, columns].astype(F32)
        v_i = val[1, k, :, columns].astype(F32)
        for b in range(vectors):
            re = slice(2 * b * nv, (2 * b + 1) * nv)
            im = slice((2 * b + 1) * nv, (2 * b + 2) * nv)
            g_r = by_r[re] - sign * by_i[im]
            g_i = by_i[re] + sign * by_r[im]
            sums[2 * b] += jnp.sum(v_r * g_r + v_i * g_i, axis=0, keepdims=True)
            sums[2 * b + 1] += jnp.sum(v_r * g_i - v_i * g_r, axis=0, keepdims=True)
            field = jnp.concatenate([g_r, g_i], axis=0).T.astype(BF16)
            for h in range(REACH):
                coefs[h, b, k] = field[h * half : (h + 1) * half]
    for row in range(2 * vectors):
        rho[row : row + 1, :] = sums[row]


def arrange_kernel(scal, *refs, entries):
    *vals, mats = refs
    for ref, entry in zip(vals, entries):
        for index, part, place in entry(scal):
            mats[part, place] = ref[index]


def potential_kernel(rho, far_rho, rows_here, rows_far, out):
    here = nt_dot(rho[...], rows_here[...], HIGHEST)
    there = nt_dot(far_rho[...], rows_far[...], HIGHEST)
    out[...] = EXCHANGE * (here + there)


def in_order(scal, mine, theirs):
    low = scal[HALF] == 0
    return jnp.concatenate([jnp.where(low, mine, theirs), jnp.where(low, theirs, mine)], axis=1)


def screened_kernel(scal, classes, *refs, tile, rows):
    reach = REACH
    groups = 3
    count = groups * reach
    coefs = refs[:count]
    mats, screen, *outs, orbs, pairs, sums, backs = refs[count:]
    _, vectors, kpts, half, width = coefs[0].shape
    nv = width // 2
    points = screen.shape[3]
    total = classes.shape[1]
    block_at = [
        place * reach + (scal[HALF] if same == 0 else reach - 1 - scal[HALF])
        for place in (1, 0, 2)
        for same in range(reach)
    ]
    top = pl.multiple_of(scal[HALF] * half, half)
    widest = (reach + 1) * kpts - 1
    class_of = {d: classes[0, lax.rem(scal[BASE] - d + total, total)] for d in range(-widest, widest + 1)}

    def column(step, carry):
        left = pl.ds(pl.multiple_of(step * tile, tile), tile)
        for n in range(count):
            for k in range(kpts):
                p = block_at[n] * kpts + k
                v_r = mats[0, p, :, left]
                v_i = mats[1, p, :, left]
                orbs[p, :nv, :tile] = v_r
                orbs[p, :nv, tile:] = -v_i
                orbs[p, nv:, :tile] = v_i
                orbs[p, nv:, tile:] = v_r
                coef = coefs[n][scal[HALF], :, k].reshape(vectors * half, width)
                pairs[p] = jnp.dot(coef, orbs[p], preferred_element_type=F32).astype(BF16)

        def chunk(index, carry):
            row = pl.multiple_of(index * rows, rows)
            w_r = {d: screen[class_of[d], 0, pl.ds(top + row, rows), left] for d in class_of}
            w_i = {d: screen[class_of[d], 1, pl.ds(top + row, rows), left] for d in class_of}
            for b in range(vectors):
                place = pl.ds(pl.multiple_of(b * half + row, rows), rows)
                m_r = [pairs[p, place, :tile] for p in range(count * kpts)]
                m_i = [pairs[p, place, tile:] for p in range(count * kpts)]
                for point in range(reach * kpts):
                    here = reach * kpts + point
                    block = here // kpts
                    real = imag = None
                    for part in (0, 1):
                        part_r = part_i = None
                        for p in range((block - reach) * kpts, (block + reach + 1) * kpts):
                            if p % 2 != part:
                                continue
                            d = here - p
                            t_r = w_r[d] * m_r[p] - w_i[d] * m_i[p]
                            t_i = w_r[d] * m_i[p] + w_i[d] * m_r[p]
                            part_r = t_r if part_r is None else part_r + t_r
                            part_i = t_i if part_i is None else part_i + t_i
                        part_r = part_r.astype(F32)
                        part_i = part_i.astype(F32)
                        real = part_r if real is None else real + part_r
                        imag = part_i if imag is None else imag + part_i
                    sums[point, place, :tile] = real.astype(BF16)
                    sums[point, place, tile:] = imag.astype(BF16)
            return carry

        lax.fori_loop(0, half // rows, chunk, 0)
        for point in range(reach * kpts):
            made = nt_dot(sums[point], orbs[reach * kpts + point])
            backs[point] = jnp.where(step == 0, made, backs[point] + made)
        return carry

    lax.fori_loop(0, points // tile, column, 0)
    for same in range(reach):
        block = scal[HALF] if same == 0 else reach - 1 - scal[HALF]
        for k in range(kpts):
            outs[same][:, k] = backs[block * kpts + k].reshape(vectors, half, width).astype(BF16)


def output_kernel(scal, own, got, cond, val, potential, keep, send):
    vectors, kpts, half, width = own.shape
    nv = width // 2
    mu = REACH * half
    share = keep.shape[4]
    side = scal[SIDE] == 0
    columns = pl.ds(pl.multiple_of(scal[SIDE] * mu, mu), mu)
    for k in range(kpts):
        v_r = val[0, k, :, columns].astype(F32)
        v_i = val[1, k, :, columns].astype(F32)
        fields = []
        for b in range(vectors):
            u_r = potential[2 * b : 2 * b + 1]
            u_i = potential[2 * b + 1 : 2 * b + 2]
            back = in_order(scal, own[b, k].astype(F32).T, got[b, k].astype(F32).T)
            fields += [u_r * v_r - u_i * v_i - back[:nv], u_r * v_i + u_i * v_r - back[nv:]]
        field = jnp.concatenate(fields, axis=0).astype(BF16)
        by_r = nt_dot(field, cond[0, k])
        by_i = nt_dot(field, cond[1, k])
        for b in range(vectors):
            re = slice(2 * b * nv, (2 * b + 1) * nv)
            im = slice((2 * b + 1) * nv, (2 * b + 2) * nv)
            for ri, out in ((0, by_r[re] + by_i[im]), (1, by_r[im] - by_i[re])):
                left, right = out[:, :share], out[:, share:]
                keep[b, ri, k] = jnp.where(side, left, right)
                send[b, ri, k] = jnp.where(side, right, left).astype(BF16)


def finish_kernel(scal, amps, energy, keep, got, out):
    vectors, _, kpts, _, share = keep.shape
    sign = jnp.where(scal[SECOND] == 1, -1.0, 1.0).astype(F32)
    columns = pl.ds(pl.multiple_of(scal[SIDE] * share, share), share)
    for k in range(kpts):
        at = scal[MIRROR + k]
        for b in range(vectors):
            for ri in range(2):
                z = amps[b, ri, at, :, columns].astype(F32)
                rest = keep[b, ri, k] + got[b, ri, k].astype(F32)
                rest = sign * rest if ri == 1 else rest
                out[b, ri, at] = (energy[k] * z + rest).astype(BF16)


def visiting_valence(valence, piece):
    kpts = valence.shape[1]
    arrays, entries = [], []

    def add(array, entry):
        arrays.append(array)
        entries.append(entry)

    def whole(same, place):
        def entry(scal):
            core = scal[HALF] if same else REACH - 1 - scal[HALF]
            block = place * REACH + core
            return [((r, k), r, block * kpts + k) for r in range(2) for k in range(kpts)]

        return entry

    def single(same, by_y):
        def entry(scal):
            core = scal[HALF] if same else REACH - 1 - scal[HALF]
            k = 1 - scal[SIDE] if by_y else scal[SIDE]
            return [
                ((slot, part), part, (2 * place * REACH + core) * kpts + k)
                for slot, place in ((0, scal[SECOND]), (1, 1 - scal[SECOND]))
                for part in range(2)
            ]

        return entry

    count = lax.axis_size("ka")
    hops = [(i, (i + REACH) % count) for i in range(count)]
    hops += [(count + i, count + (i - REACH) % count) for i in range(count)]
    mine = lax.ppermute(piece, ("pm", "ka"), hops)
    other = exchanged(mine, "pm", 1)
    add(valence, whole(True, 1))
    add(exchanged(valence, "ka", 1), whole(False, 1))
    (both,) = call(stack_kernel, [], [mine, other], [((2, *piece.shape), BF16)])
    across = exchanged(both, "isdf", 1)
    for by_y, array in ((False, both), (True, across)):
        add(array, single(True, by_y))
        add(exchanged(array, "ka", 1), single(False, by_y))
    return arrays, entries


def call(body, scalars, operands, shapes, scratch=(), limit=8, space=VMEM):
    return pl.pallas_call(
        body,
        in_specs=[SMEM] * len(scalars) + [space] * len(operands),
        out_specs=[VMEM] * len(shapes),
        out_shape=[jax.ShapeDtypeStruct(*shape) for shape in shapes],
        scratch_shapes=list(scratch),
        compiler_params=pltpu.CompilerParams(vmem_limit_bytes=limit << 20),
    )(*scalars, *operands)


def per_device(amplitudes, conduction, valence, energy, screened, coulomb, mirror, transfer_class):
    second = lax.axis_index("pm")
    ka_index = lax.axis_index("ka")
    isdf_index = lax.axis_index("isdf")
    ka_count = lax.axis_size("ka")
    kpts, _, mu = conduction.shape[1:]
    nv, points = valence.shape[2:]
    share = energy.shape[2]
    vectors = amplitudes.shape[1]
    half = mu // REACH
    width = 2 * nv
    hbm = pl.BlockSpec(memory_space=pltpu.MemorySpace.HBM)

    far = mirrored(amplitudes[0])
    conduction, valence, piece = call(
        share_kernel,
        [],
        [conduction, valence],
        [(conduction.shape, BF16), (valence.shape, BF16), ((2, nv, points), BF16)],
        [pltpu.SemaphoreType.DMA((3,))],
        space=hbm,
    )
    visiting, entries = visiting_valence(valence, piece)

    partner = jnp.clip(mirror - (ka_count - 1 - ka_index) * kpts, 0, kpts - 1)
    local = jnp.where(second == 1, partner, jnp.arange(kpts, dtype=jnp.int32))
    places = jnp.stack([second, ka_index * kpts, ka_index % REACH, isdf_index])
    scal = jnp.concatenate([places.astype(jnp.int32), local.astype(jnp.int32)])

    coef_shape = ((REACH, vectors, kpts, half, width), BF16)
    own, total = call(
        coef_kernel, [scal], [far, conduction, valence], [coef_shape, ((2 * vectors, mu), F32)]
    )
    below = group_shift(own, 1)
    above = group_shift(own, -1)
    coefs = []
    for value in (own, below, above):
        coefs += [value, exchanged(value, "ka", 1)]

    total = total + exchanged(total, "ka", 1)
    if ka_count // REACH == 4:
        others = [group_shift(total, shift) for shift in (1, 3, 2)]
        total = (total + others[2]) + (others[0] + others[1])
    else:
        bit = REACH
        while bit < ka_count:
            total = total + exchanged(total, "ka", bit)
            bit *= 2
    total = total + exchanged(total, "pm", 1)
    far_total = exchanged(total, "isdf", 1)
    rows_here = lax.dynamic_slice_in_dim(coulomb, isdf_index * mu, mu, 0)
    rows_there = lax.dynamic_slice_in_dim(coulomb, (1 - isdf_index) * mu, mu, 0)
    rows_far = exchanged(rows_there, "isdf", 1)
    (potential,) = call(
        potential_kernel, [], [total, far_total, rows_here, rows_far], [((2 * vectors, mu), F32)]
    )
    (mats,) = call(
        functools.partial(arrange_kernel, entries=entries),
        [scal],
        visiting,
        [((2, 3 * REACH * kpts, nv, points), BF16)],
        limit=12,
    )

    tile = 128
    back_shape = ((vectors, kpts, half, width), BF16)
    out_shape = (vectors, 2, kpts, nv, share)
    mine, theirs = call(
        functools.partial(screened_kernel, tile=tile, rows=16),
        [scal, transfer_class],
        [*coefs, mats, screened],
        [back_shape, back_shape],
        [
            pltpu.VMEM((3 * REACH * kpts, width, 2 * tile), BF16),
            pltpu.VMEM((3 * REACH * kpts, vectors * half, 2 * tile), BF16),
            pltpu.VMEM((REACH * kpts, vectors * half, 2 * tile), BF16),
            pltpu.VMEM((REACH * kpts, vectors * half, width), F32),
        ],
        limit=16,
    )
    got = exchanged(theirs, "ka", 1)
    out_keep, out_send = call(
        output_kernel,
        [scal],
        [mine, got, conduction, valence, potential],
        [(out_shape, F32), (out_shape, BF16)],
    )
    out_got = exchanged(out_send, "isdf", 1)
    (channel,) = call(finish_kernel, [scal], [far, energy, out_keep, out_got], [(out_shape, BF16)])
    result = mirrored(channel)
    return result[None]


def solution(mesh):
    return jax.shard_map(
        per_device,
        mesh=mesh,
        in_specs=(
            P("pm", None, None, "ka", None, None),
            P(None, "ka", None, "isdf"),
            P(None, "ka", None, None),
            P("ka", None, "isdf"),
            P(None, None, "isdf", None),
            P(None, "isdf"),
            P("ka"),
            P("ka", None),
        ),
        out_specs=P("pm", None, None, "ka", None, "isdf"),
        check_vma=False,
    )
```
